32 devices in a mesh: band: 16 (over z, x, core), lev: 2 (over y).
Axes of the slice: x: 2, y: 2, z: 4, core: 2. Of those that a mesh axis runs over, the one named last changes fastest.
Arguments:
- field_grid: float32 [3, 8, 384, 2, 1536], P(None, 'lev', 'band'), may hold values from -6 to 6
- increment: float32 [3, 8, 384, 2, 1536], P(None, 'lev', 'band'), may hold values from -6 to 6
- points: int32 [384], P('band'), may hold values from 16 to 1536, as said below
- weights: float32 [384], replicated, may hold values from 0.0013020834 to 0.0052083335
- pair_slot: int32 [384], replicated, may hold values from 0 to 383, each once
- legendre: float32 [384, 384, 769], P(('band', 'lev')), may hold values from -6 to 6
- strength: float32 [3, 8], replicated, may hold values from 1 to 16
Outputs:
- stepped: float32 [3, 8, 384, 2, 1536], P(None, 'lev', 'band')
The draws below stay inside these ranges and needn't reach their ends.
Inputs may be any that keep to these rules, and one draw needn't show every extreme that they name: points[j] lies within 32 of 16 + 1520 * j // 383, kept within 16 to 1536; the last latitude pair has 1536 cells. `pair_slot`: A permutation of 0 to 383; slot s is held by the device of joint band+lev index s // 12, at place s % 12, which holds legendre[s].
All inputs are finite; a program needn't handle non-finite values.
Results may differ from the reference program's by a relative error of at most 0.0003.
Values sent between devices are 32-bit elements; how exact they have to be, the bound alone decides.
A program may use at most 320 MiB of HBM per device.

```python
import math
import jax
import jax.numpy as jnp
from jax import lax

WAVES = 768
FIELDS = 3
HALF = 384
NLON = 1536
LEVELS = 8


def draw_points(key, part):
    pair_index = lax.iota(jnp.int32, HALF)
    smooth_count = 16 + (2 * WAVES - 16) * pair_index // (HALF - 1)
    jitter = jax.random.randint(key, (HALF,), -32, 33)
    counts = jnp.clip(smooth_count + jitter, 16, 2 * WAVES)
    return jnp.where(pair_index == HALF - 1, 2 * WAVES, counts).astype(jnp.int32)


def levels(own_key, dims, cuts, least, high):
    level, own = 1.0, jax.random.fold_in(own_key, 6)
    for position, shards_of in cuts:
        draws = jnp.exp(jax.random.uniform(jax.random.fold_in(own, position), (shards_of,), jnp.float32, least / len(cuts), high / len(cuts)))
        level = level * jnp.repeat(draws, dims[position] // shards_of).reshape([-1 if axis == position else 1 for axis in range(len(dims))])
    return level


def normal_values(rng, shape, spread, bound, cuts=(), kind=jnp.bfloat16):
    entries = jax.random.normal(rng, shape, jnp.float32) * spread
    if len(cuts) > 0:
        entries = levels(rng, shape, cuts, -0.22, 0.18) * entries
    return jnp.clip(entries, min=-bound, max=bound).astype(kind)


def setup_inputs(seed: int = 0) -> dict:
    arg_keys = jax.random.split(jax.random.key(seed), 8)
    return {
        "field_grid": normal_values(arg_keys[0], (FIELDS, LEVELS, HALF, 2, NLON), 1.0, 6.0, ((1, 2), (2, 16)), jnp.float32),
        "increment": normal_values(arg_keys[1], (FIELDS, LEVELS, HALF, 2, NLON), 1.0, 6.0, ((1, 2), (2, 16)), jnp.float32),
        "points": draw_points(jax.random.fold_in(arg_keys[7], 71), 0),
        "weights": jnp.clip(jnp.exp(jax.random.uniform(arg_keys[3], (HALF,), jnp.float32, math.log(0.0013020834), math.log(0.0052083335))), 0.0013020834, 0.0052083335),
        "pair_slot": jax.random.permutation(arg_keys[4], HALF).astype(jnp.int32),
        "legendre": normal_values(arg_keys[5], (HALF, HALF, WAVES + 1), 1.0, 6.0, ((0, 32),), jnp.float32),
        "strength": jnp.clip(jnp.exp(jax.random.uniform(arg_keys[6], (FIELDS, LEVELS), jnp.float32, math.log(1.0), math.log(16.0))), 1.0, 16.0),
    }


TWO_PI = 2.0 * math.pi


def dft_basis(count):
    places = lax.iota(jnp.int32, NLON)
    orders = lax.iota(jnp.int32, WAVES)
    turns = (places[:, None] * orders[None, :]) % count
    angle = turns.astype(jnp.float32) * (TWO_PI / count.astype(jnp.float32))
    live = (places[:, None] < count) & (orders[None, :] <= (count - 1) // 2)
    cosines = jnp.where(live, jnp.cos(angle), 0.0)
    sines = jnp.where(live, -jnp.sin(angle), 0.0)
    return jnp.concatenate([cosines, sines], axis=1)


def reference(field_grid, increment, points, weights, pair_slot, legendre, strength):
    summed = field_grid + increment
    row_count = FIELDS * LEVELS * 2
    by_pair = jnp.moveaxis(summed, 2, 0).reshape(HALF, row_count, NLON)

    def forward(item):
        block, count = item
        product = jnp.dot(block, dft_basis(count), precision=lax.Precision.HIGHEST)
        return product / count.astype(jnp.float32)

    spectra = lax.map(forward, (by_pair, points))
    spectra = spectra.reshape(HALF, FIELDS * LEVELS, 2, 2, WAVES)
    columns = lax.iota(jnp.int32, WAVES + 1)
    degree_top = float((WAVES - 1) * WAVES)
    damping_rate = strength.reshape(FIELDS * LEVELS)

    def per_pair(lower_wave):
        table = lax.dynamic_index_in_dim(legendre, pair_slot[lower_wave], 0, keepdims=False)
        higher_wave = WAVES - 1 - lower_wave
        first = lax.dynamic_index_in_dim(spectra, lower_wave, 4, keepdims=False)
        second = lax.dynamic_index_in_dim(spectra, higher_wave, 4, keepdims=False)
        second_member = columns >= WAVES - lower_wave
        degree = jnp.where(second_member, columns - 1, lower_wave + columns)
        wave_of_column = jnp.where(second_member, higher_wave, lower_wave)
        parity = jnp.where((degree - wave_of_column) % 2 == 0, 1.0, -1.0)
        first_weighted = (first * weights[:, None, None, None]).reshape(HALF, -1)
        second_weighted = (second * weights[:, None, None, None]).reshape(HALF, -1)
        part_first = jnp.dot(table.T, first_weighted, precision=lax.Precision.HIGHEST)
        part_second = jnp.dot(table.T, second_weighted, precision=lax.Precision.HIGHEST)
        part_first = part_first.reshape(WAVES + 1, FIELDS * LEVELS, 2, 2)
        part_second = part_second.reshape(WAVES + 1, FIELDS * LEVELS, 2, 2)
        chosen = jnp.where(second_member[:, None, None, None], part_second, part_first)
        coefficients = chosen[:, :, 0, :] + parity[:, None, None] * chosen[:, :, 1, :]
        degree_real = degree.astype(jnp.float32)
        degree_ratio = degree_real * (degree_real + 1.0) / degree_top
        damping = 1.0 / (1.0 + damping_rate[None, :] * (degree_ratio * degree_ratio)[:, None])
        damped = coefficients * damping[:, :, None]
        lower_part = jnp.where(second_member[:, None, None], 0.0, damped)
        upper_part = jnp.where(second_member[:, None, None], damped, 0.0)
        stacked = jnp.stack([lower_part, lower_part * parity[:, None, None],
                             upper_part, upper_part * parity[:, None, None]], axis=1)
        returned = jnp.dot(table, stacked.reshape(WAVES + 1, -1), precision=lax.Precision.HIGHEST)
        returned = returned.reshape(HALF, 2, 2, FIELDS * LEVELS, 2)
        return returned[:, 0], returned[:, 1]

    first_back, second_back = lax.map(per_pair, lax.iota(jnp.int32, HALF))
    by_wave = jnp.concatenate([first_back, second_back[::-1]], axis=0)
    spectral_rows = jnp.transpose(by_wave, (1, 3, 2, 4, 0)).reshape(HALF, row_count, 2 * WAVES)
    doubling = jnp.where(lax.iota(jnp.int32, 2 * WAVES) % WAVES == 0, 1.0, 2.0)

    def inverse(item):
        block, count = item
        return jnp.dot(block * doubling[None, :], dft_basis(count).T, precision=lax.Precision.HIGHEST)

    grid_rows = lax.map(inverse, (spectral_rows, points))
    grid_rows = grid_rows.reshape(HALF, FIELDS, LEVELS, 2, NLON)
    return jnp.moveaxis(grid_rows, 0, 2)
```

```python
import math

import jax
import jax.numpy as jnp
from jax import lax
from jax.experimental import pallas as pl
from jax.experimental.pallas import tpu as pltpu
from jax.sharding import PartitionSpec as P

TWO_PI = 2.0 * math.pi


INNER = 32
CHUNK = 256


def dft_factors(counts, length, wavecount):
    orders = lax.iota(jnp.int32, wavecount)
    coarse = lax.iota(jnp.int32, length // INNER) * INNER
    finer = lax.iota(jnp.int32, INNER)
    places = jnp.concatenate([coarse, finer])
    step_angle = (TWO_PI / counts.astype(jnp.float32))[:, None, None]
    turns = places[None, :, None] * orders[None, None, :] % counts[:, None, None]
    angle = turns.astype(jnp.float32) * step_angle
    cosines, sines = jnp.cos(angle), jnp.sin(angle)
    split = length // INNER
    return cosines[:, :split], sines[:, :split], cosines[:, split:], sines[:, split:]


def halves(values):
    high = values.astype(jnp.bfloat16)
    return high, (values - high.astype(jnp.float32)).astype(jnp.bfloat16)


def build_chunk(coarse_cos, coarse_sin, finer_cos, finer_sin, high_ref, low_ref):
    waves = finer_cos.shape[2]
    fine_cos, fine_sin = finer_cos[0], finer_sin[0]
    for step in range(CHUNK // INNER):
        step_cos = coarse_cos[0, step : step + 1, :]
        step_sin = coarse_sin[0, step : step + 1, :]
        rows = pl.ds(step * INNER, INNER)
        high, low = halves(step_cos * fine_cos - step_sin * fine_sin)
        high_ref[rows, :waves] = high
        low_ref[rows, :waves] = low
        high, low = halves(-(step_sin * fine_cos + step_cos * fine_sin))
        high_ref[rows, waves:] = high
        low_ref[rows, waves:] = low


def split_dot(values, high_ref, low_ref, contract):
    rows = values.shape[0]
    high, low = halves(values)
    dims = (((1,), (contract,)), ((), ()))
    both = lax.dot_general(
        jnp.concatenate([high, low], axis=0), high_ref[...], dims,
        preferred_element_type=jnp.float32,
    )
    rest = lax.dot_general(high, low_ref[...], dims, preferred_element_type=jnp.float32)
    return both[:rows] + (both[rows:] + rest)


def forward_kernel(counts, rows_ref, cc, cs, fc, fs, out_ref, total, high_ref, low_ref):
    pair, step = pl.program_id(0), pl.program_id(1)
    count = counts[pair]
    waves = fc.shape[2]

    @pl.when(step == 0)
    def _():
        total[...] = jnp.zeros_like(total)

    @pl.when(step * CHUNK < count)
    def _():
        build_chunk(cc, cs, fc, fs, high_ref, low_ref)
        block = rows_ref[0]
        place = step * CHUNK + lax.broadcasted_iota(jnp.int32, block.shape, 1)
        block = jnp.where(place < count, block, 0.0)
        total[...] += split_dot(block, high_ref, low_ref, 0)

    @pl.when(step == pl.num_programs(1) - 1)
    def _():
        scale_count = count.astype(jnp.float32)
        order = lax.broadcasted_iota(jnp.int32, (total.shape[0], waves), 1)
        live = order <= (count - 1) // 2
        out_ref[0, 0] = jnp.where(live, total[:, :waves], 0.0) / scale_count
        out_ref[0, 1] = jnp.where(live, total[:, waves:], 0.0) / scale_count


def inverse_kernel(counts, rows_ref, cc, cs, fc, fs, out_ref, high_ref, low_ref):
    pair, step = pl.program_id(0), pl.program_id(1)
    count = counts[pair]
    waves = fc.shape[2]

    @pl.when(step * CHUNK >= count)
    def _():
        out_ref[...] = jnp.zeros_like(out_ref)

    @pl.when(step * CHUNK < count)
    def _():
        build_chunk(cc, cs, fc, fs, high_ref, low_ref)
        order = lax.broadcasted_iota(jnp.int32, (rows_ref.shape[2], waves), 1)
        doubling = jnp.where(order == 0, 1.0, 2.0)
        doubling = jnp.where(order <= (count - 1) // 2, doubling, 0.0)
        values = jnp.concatenate([rows_ref[0, 0] * doubling, rows_ref[0, 1] * doubling], axis=1)
        result = split_dot(values, high_ref, low_ref, 1)
        place = step * CHUNK + lax.broadcasted_iota(jnp.int32, result.shape, 1)
        out_ref[0] = jnp.where(place < count, result, 0.0)


def transform(counts, rows, factors, length, wavecount, inverse):
    pairs = counts.shape[0]
    row_count = rows.shape[2] if inverse else rows.shape[1]
    grid_spec_ = pl.BlockSpec((1, row_count, CHUNK), lambda p, k, c: (p, 0, k))
    wave_spec = pl.BlockSpec((1, 2, row_count, wavecount), lambda p, k, c: (p, 0, 0, 0))
    coarse = pl.BlockSpec((1, CHUNK // INNER, wavecount), lambda p, k, c: (p, k, 0))
    finer = pl.BlockSpec((1, INNER, wavecount), lambda p, k, c: (p, 0, 0))
    table = pltpu.VMEM((CHUNK, 2 * wavecount), jnp.bfloat16)
    total = [] if inverse else [pltpu.VMEM((row_count, 2 * wavecount), jnp.float32)]
    shape = (pairs, row_count, length) if inverse else (pairs, 2, row_count, wavecount)
    flops = 6 * pairs * row_count * length * 2 * wavecount
    return pl.pallas_call(
        inverse_kernel if inverse else forward_kernel,
        out_shape=jax.ShapeDtypeStruct(shape, jnp.float32),
        grid_spec=pltpu.PrefetchScalarGridSpec(
            num_scalar_prefetch=1,
            grid=(pairs, length // CHUNK),
            in_specs=[wave_spec if inverse else grid_spec_, coarse, coarse, finer, finer],
            out_specs=grid_spec_ if inverse else wave_spec,
            scratch_shapes=total + [table, table],
        ),
        cost_estimate=pl.CostEstimate(
            flops=flops, bytes_accessed=8 * pairs * row_count * length, transcendentals=0
        ),
    )(counts, rows, *factors)


def body(field_grid, increment, points, weights, pair_slot, legendre, strength):
    band_count = lax.axis_size("band")
    level_groups = lax.axis_size("lev")
    summed = field_grid + increment
    fields = summed.shape[0]
    local_levels = summed.shape[1]
    band_pairs = summed.shape[2]
    length = summed.shape[4]
    wavecount = length // 2
    pair_total = wavecount // 2
    total_levels = local_levels * level_groups
    regrouped = lax.all_to_all(summed, "lev", split_axis=2, concat_axis=1, tiled=True)
    piece_pairs = band_pairs // level_groups
    counts = lax.dynamic_slice_in_dim(points, lax.axis_index("lev") * piece_pairs, piece_pairs)
    factors = dft_factors(counts, length, wavecount)
    row_count = fields * total_levels * 2
    pair_rows = jnp.moveaxis(regrouped, 2, 0).reshape(piece_pairs, row_count, length)
    spectra = transform(counts, pair_rows, factors, length, wavecount, False)
    piece_width = 2 * row_count
    by_wave = spectra.reshape(piece_pairs * piece_width, wavecount).T
    slot_ranks = lax.iota(jnp.int32, pair_total)
    pair_of_slot = jnp.zeros((pair_total,), jnp.int32).at[pair_slot].set(slot_ranks)
    wave_order = jnp.stack([pair_of_slot, wavecount - 1 - pair_of_slot], axis=1).reshape(wavecount)
    outgoing = jnp.take(by_wave, wave_order, axis=0)
    slot_count = legendre.shape[0]
    device_count = band_count * level_groups
    arrived = lax.all_to_all(outgoing, ("band", "lev"), split_axis=0, concat_axis=0, tiled=True)
    arrived = arrived.reshape(device_count, 2 * slot_count, piece_pairs, piece_width)
    arrived = jnp.transpose(arrived, (1, 0, 2, 3))
    row_width = 4 * fields * total_levels
    arrived = arrived.reshape(2 * slot_count, pair_total, row_width)
    lat_count = arrived.shape[1]
    own_slots = lax.axis_index(("band", "lev")) * slot_count + lax.iota(jnp.int32, slot_count)
    lower_wave = jnp.take(pair_of_slot, own_slots)
    columns = lax.iota(jnp.int32, wavecount + 1)
    second_member = columns[None, :] >= (wavecount - lower_wave)[:, None]
    degree = jnp.where(second_member, columns[None, :] - 1, lower_wave[:, None] + columns[None, :])
    wave_of_column = jnp.where(
        second_member, wavecount - 1 - lower_wave[:, None], lower_wave[:, None]
    )
    parity = jnp.where((degree - wave_of_column) % 2 == 0, 1.0, -1.0)
    weighted = arrived.reshape(slot_count, 2, lat_count, row_width) * weights[None, None, :, None]
    analysed = jnp.einsum("sjc,sejr->scer", legendre, weighted, precision=lax.Precision.HIGH)
    analysed = analysed.reshape(slot_count, wavecount + 1, 2, 2, fields * total_levels, 2)
    chosen = jnp.where(second_member[:, :, None, None, None], analysed[:, :, 1], analysed[:, :, 0])
    coefficients = chosen[..., 0] + parity[:, :, None, None] * chosen[..., 1]
    degree_real = degree.astype(jnp.float32)
    degree_ratio = degree_real * (degree_real + 1.0) / float((wavecount - 1) * wavecount)
    damping_rate = strength.reshape(fields * total_levels)
    damping = 1.0 / (1.0 + damping_rate[None, None, :] * (degree_ratio * degree_ratio)[:, :, None])
    damped = coefficients * damping[:, :, None, :]
    second_real = jnp.where(second_member, 1.0, 0.0)
    member_mask = jnp.stack([1.0 - second_real, second_real], axis=2)
    hemisphere_sign = jnp.stack([jnp.ones_like(parity), parity], axis=2)
    spread = damped[:, :, None, :, :, None] * member_mask[:, :, :, None, None, None]
    spread = spread * hemisphere_sign[:, :, None, None, None, :]
    spread = spread.reshape(slot_count, wavecount + 1, 2 * row_width)
    returned = jnp.einsum("sjc,scr->sjr", legendre, spread, precision=lax.Precision.HIGH)
    leaving = returned.reshape(slot_count, device_count, piece_pairs, 2, row_width)
    leaving = jnp.transpose(leaving, (1, 0, 3, 2, 4))
    leaving = leaving.reshape(wavecount, piece_pairs * piece_width)
    home_rows = lax.all_to_all(leaving, ("band", "lev"), split_axis=0, concat_axis=0, tiled=True)
    positions = (
        jnp.zeros((wavecount,), jnp.int32).at[wave_order].set(lax.iota(jnp.int32, wavecount))
    )
    restored = jnp.take(home_rows, positions, axis=0)
    spectral_rows = restored.T.reshape(piece_pairs, 2, row_count, wavecount)
    grid_rows = transform(counts, spectral_rows, factors, length, wavecount, True)
    grid_rows = jnp.moveaxis(grid_rows.reshape(piece_pairs, fields, total_levels, 2, length), 0, 2)
    return lax.all_to_all(grid_rows, "lev", split_axis=1, concat_axis=2, tiled=True)


def solution(mesh):
    return jax.shard_map(
        body,
        mesh=mesh,
        in_specs=(
            P(None, "lev", "band", None, None),
            P(None, "lev", "band", None, None),
            P("band"),
            P(),
            P(),
            P(("band", "lev"), None, None),
            P(),
        ),
        out_specs=P(None, "lev", "band", None, None),
        check_vma=False,
    )
```
